32 devices in a mesh: vocab: 8 (over z, x), dp: 4 (over y, core).
Axes of the slice: x: 2, y: 2, z: 4, core: 2. Of those that a mesh axis runs over, the one named last changes fastest.
Arguments:
- teacher_hidden: bfloat16 [512, 5376], P('dp'), may hold values from -48 to 48
- student_hidden: bfloat16 [512, 2560], P('dp'), may hold values from -48 to 48
- teacher_codes: bfloat16 [16384, 5376], P(('vocab', 'dp')), may hold values from -8 to 7, as said below
- teacher_scales: float32 [16384, 42], P(('vocab', 'dp')), may hold values from 0.003 to 0.07
- student_weight: bfloat16 [16384, 2560], P(('vocab', 'dp')), may hold values from -1 to 1
- loss_scale: bfloat16 [512], P('dp'), may hold values from 2 to 20
Outputs:
- kl: float32 [512], P('dp')
- grad_hidden: bfloat16 [512, 2560], P('dp', 'vocab')
- grad_weight: bfloat16 [16384, 2560], P(('vocab', 'dp'))
The draws below stay inside these ranges and needn't reach their ends.
Inputs may be any that keep to these rules, and one draw needn't show every extreme that they name: `teacher_codes`: whole numbers.
All inputs are finite; a program needn't handle non-finite values.
Results may differ from the reference program's by a relative error of at most 0.0085.
Values may be sent and summed in bfloat16 or wider, within the bound.
A program may use at most 128 MiB of HBM per device.

```python
import math
import jax
import jax.numpy as jnp
from jax import lax

DT = 5376
DS = 2560
GROUP = 128
V_DEV = 512
TOKENS = 512
VOCAB = 16384
N_VOCAB = 8
N_DP = 4


def code_rows(key, row_ids):
    base_key = jax.random.fold_in(key, 101)

    def single(row_id):
        return jax.random.randint(jax.random.fold_in(base_key, row_id), (DT,), -8, 8).astype(jnp.float32)
    return jax.vmap(single)(row_ids)


def scale_rows(key, row_ids):
    base_key = jax.random.fold_in(key, 202)
    level_low, level_high, rise_total = (0.0085, 0.0105, 1.1)

    def single(row_id):
        key_pair = jax.random.split(jax.random.fold_in(base_key, row_id))
        scale_level = jnp.exp(jax.random.uniform(key_pair[0], (), jnp.float32, math.log(level_low), math.log(level_high)))
        jitter_factor = jnp.exp(jax.random.uniform(key_pair[1], (DT // GROUP,), jnp.float32, math.log(0.8), math.log(1.25)))
        rising_factor = jnp.exp(math.log(rise_total) * row_id.astype(jnp.float32) / VOCAB)
        return scale_level * rising_factor * jitter_factor
    return jax.vmap(single)(row_ids)


def student_rows(key, row_ids):
    base_key = jax.random.fold_in(key, 303)
    level_low, level_high, rise_total = (0.9, 1.2, 1.5)

    def single(row_id):
        key_pair = jax.random.split(jax.random.fold_in(base_key, row_id))
        scale_level = jnp.exp(jax.random.uniform(key_pair[0], (), jnp.float32, math.log(level_low), math.log(level_high)))
        rising_factor = jnp.exp(math.log(rise_total) * row_id.astype(jnp.float32) / VOCAB)
        values = jnp.clip(jax.random.normal(key_pair[1], (DS,), jnp.float32), -4.0, 4.0)
        return jnp.clip(scale_level * rising_factor * values / math.sqrt(DS), -1.0, 1.0)
    return jax.vmap(single)(row_ids).astype(jnp.bfloat16).astype(jnp.float32)


def hidden_draw(key, col_count, salt_value):
    key_list = jax.random.split(jax.random.fold_in(key, salt_value), 2)
    row_scale = jnp.exp(jax.random.uniform(key_list[0], (TOKENS, 1), jnp.float32, math.log(0.9), math.log(1.1)))
    values = jax.random.normal(key_list[1], (TOKENS, col_count), jnp.float32) * row_scale
    return jnp.clip(values, -48.0, 48.0).astype(jnp.bfloat16)


def draw_teacher_hidden(key, part):
    return hidden_draw(key, DT, 505)


def draw_student_hidden(key, part):
    return hidden_draw(key, DS, 606)


def draw_teacher_codes(key, part):
    return code_rows(key, jnp.arange(VOCAB, dtype=jnp.int32)).astype(jnp.bfloat16)


def draw_teacher_scales(key, part):
    return scale_rows(key, jnp.arange(VOCAB, dtype=jnp.int32)).astype(jnp.float32)


def draw_student_weight(key, part):
    return student_rows(key, jnp.arange(VOCAB, dtype=jnp.int32)).astype(jnp.bfloat16)


def steps_of(key, dims, pieces, least, largest):
    gain = 1.0
    for dim, blocks in pieces:
        steps = jax.random.uniform(jax.random.fold_in(jax.random.fold_in(key, 6), dim), (blocks,), jnp.float32, least / len(pieces), largest / len(pieces))
        gain = gain * jnp.repeat(jnp.exp(steps), dims[dim] // blocks).reshape((-1,) + (1,) * (len(dims) - 1 - dim))
    return gain


def setup_inputs(seed: int = 0) -> dict:
    seeds = jax.random.split(jax.random.key(seed), 7)
    return {
        "teacher_hidden": draw_teacher_hidden(jax.random.fold_in(seeds[6], 71), 0),
        "student_hidden": draw_student_hidden(jax.random.fold_in(seeds[6], 71), 0),
        "teacher_codes": draw_teacher_codes(jax.random.fold_in(seeds[6], 71), 0),
        "teacher_scales": draw_teacher_scales(jax.random.fold_in(seeds[6], 71), 0),
        "student_weight": draw_student_weight(jax.random.fold_in(seeds[6], 71), 0),
        "loss_scale": jnp.clip(jnp.exp(math.log(20.0) - 2.3025851 * jax.random.uniform(seeds[5], (TOKENS,), jnp.float32) ** steps_of(seeds[5], (TOKENS,), ((0, 4),), -0.2, 0.2)), 2.0, 20.0).astype(jnp.bfloat16),
    }


def dequantize(code_values, scales):
    row_count = code_values.shape[0]
    grouped = code_values.astype(jnp.float32).reshape(row_count, -1, GROUP) * scales.astype(jnp.float32)[:, :, None]
    return grouped.reshape(row_count, -1).astype(jnp.bfloat16)


def reference(teacher_hidden, student_hidden, teacher_codes, teacher_scales, student_weight, loss_scale):
    blocks = N_VOCAB * N_DP
    teacher_wide = teacher_hidden.astype(jnp.float32)
    student_wide = student_hidden.astype(jnp.float32)
    code_blocks = teacher_codes.reshape(blocks, V_DEV, DT)
    scale_blocks = teacher_scales.reshape(blocks, V_DEV, DT // GROUP)
    weight_blocks = student_weight.reshape(blocks, V_DEV, DS)

    def block_logits(members):
        code_values, scales, weight = members
        dequant_rows = dequantize(code_values, scales).astype(jnp.float32)
        teacher_part = jnp.dot(teacher_wide, dequant_rows.T, preferred_element_type=jnp.float32, precision=lax.Precision.HIGHEST)
        student_part = jnp.dot(student_wide, weight.astype(jnp.float32).T, preferred_element_type=jnp.float32, precision=lax.Precision.HIGHEST)
        return teacher_part, student_part

    teacher_logits, student_logits = lax.map(block_logits, (code_blocks, scale_blocks, weight_blocks))
    teacher_top = jnp.max(teacher_logits, axis=(0, 2))
    student_top = jnp.max(student_logits, axis=(0, 2))
    teacher_exp = jnp.exp(teacher_logits - teacher_top[None, :, None])
    teacher_total = jnp.sum(teacher_exp, axis=(0, 2))
    cross_total = jnp.sum(teacher_exp * (teacher_logits - student_logits), axis=(0, 2))
    student_total = jnp.sum(jnp.exp(student_logits - student_top[None, :, None]), axis=(0, 2))
    teacher_lse = teacher_top + jnp.log(teacher_total)
    student_lse = student_top + jnp.log(student_total)
    kl = cross_total / teacher_total - teacher_lse + student_lse
    teacher_prob = jnp.exp(teacher_logits - teacher_lse[None, :, None])
    student_prob = jnp.exp(student_logits - student_lse[None, :, None])
    logit_grad = (loss_scale.astype(jnp.float32)[None, :, None] * (student_prob - teacher_prob)).astype(jnp.bfloat16)

    def add_block(running, members):
        grad_block, weight = members
        product = jnp.dot(grad_block.astype(jnp.float32), weight.astype(jnp.float32), preferred_element_type=jnp.float32, precision=lax.Precision.HIGHEST)
        return running + product, None

    grad_hidden, unused = lax.scan(add_block, jnp.zeros((TOKENS, DS), jnp.float32), (logit_grad, weight_blocks))

    def weight_block(grad_block):
        product = jnp.dot(grad_block.astype(jnp.float32).T, student_wide, preferred_element_type=jnp.float32, precision=lax.Precision.HIGHEST)
        return product.astype(jnp.bfloat16)

    grad_weight = lax.map(weight_block, logit_grad).reshape(blocks * V_DEV, DS)
    return kl, grad_hidden.astype(jnp.bfloat16), grad_weight
```

```python
import functools

import jax
import jax.numpy as jnp
from jax import lax
from jax.experimental import pallas as pl
from jax.experimental.pallas import tpu as pltpu
from jax.sharding import PartitionSpec as P

GROUP = 128
LANE = 128
MESH = pl.DeviceIdType.MESH


def step_width(cols):
    units = cols // 256
    per = max(k for k in (1, 2, 3) if units % k == 0)
    return per * 256


def dot_t(left_rows, right_rows):
    return lax.dot_general(
        left_rows, right_rows, (((1,), (1,)), ((), ())), preferred_element_type=jnp.float32
    )


def kernel(
    n_vocab, n_dp,
    th_own, sh_own, codes, scales, weight, loss,
    kl_out, gh_out, gw_out,
    th, sh, table, wgt, wgt_t, tlog, slog, lsc, stat, stat_b, fin, in_a, in_b,
    grad, gw_buf, mine, theirs, core_in,
    y1s, y1r, x1s, x1r, x2s, x2r, y2s, y2r, zs, zr, zf,
    ld_sem, gw_sem, pc_s, pc_r, ys, yr, xs, xr, d1s, d1r, d2s, d2r,
    ls_s, ls_r, a_s, a_r, b_s, b_r, cs, cr, r1s, r1r, r2s, r2r, z_ss, z_rs,
):
    v, d = lax.axis_index("vocab"), lax.axis_index("dp")
    c, y = lax.rem(d, 2), lax.div(d, 2)
    p, q = lax.rem(v, 2), lax.div(v, 2)
    n_y, n_z = n_dp // 2, n_vocab // 2
    n_off = n_y - 1
    mate = 2 * y + 1 - c
    v_pair = 2 * q + 1 - p
    tok = th_own.shape[0]
    rv = zr.shape[1]
    n_z1 = n_z // 2

    def rcopy(src, dst, send, recv, dev):
        return pltpu.make_async_remote_copy(
            src_ref=src, dst_ref=dst, send_sem=send, recv_sem=recv,
            device_id=dev, device_id_type=MESH,
        )

    chunks = []
    for own, scr, tab, acc in ((th_own, th, table, tlog), (sh_own, sh, wgt, slog)):
        width = step_width(own.shape[1])
        for base in range(0, own.shape[1], width):
            chunks.append((own, scr, tab, acc, base, width))
    n_ch = len(chunks)

    loads = []
    for k, (own, scr, tab, acc, base, width) in enumerate(chunks):
        src = codes if tab is table else weight
        cp = pltpu.make_async_copy(
            src.at[:, pl.ds(base, width)], tab.at[:, pl.ds(base, width)], ld_sem.at[k]
        )
        cp.start()
        loads.append(cp)
    own_rows = pl.ds(pl.multiple_of(d * tok, tok), tok)
    own_loads = [
        pltpu.make_async_copy(th_own, th.at[own_rows], ld_sem.at[n_ch]),
        pltpu.make_async_copy(sh_own, sh.at[own_rows], ld_sem.at[n_ch + 1]),
    ]
    for cp in own_loads:
        cp.start()

    peers_a = []
    for dv in range(2):
        for dd in range(n_dp):
            if dv or dd:
                peers_a.append((v if dv == 0 else v_pair, lax.rem(d + dd, n_dp)))
    from_a = []
    peers_b = [(2 * lax.rem(q + o, n_z) + p, d) for o in range(1, n_z)]
    barrier = pltpu.get_barrier_semaphore()
    for peer in peers_a + peers_b:
        pl.semaphore_signal(barrier, inc=1, device_id=peer, device_id_type=MESH)
    pl.semaphore_wait(barrier, len(peers_a) + len(peers_b))

    def cols(k, which):
        base, width = chunks[k][4], chunks[k][5]
        half = width // 2
        return pl.ds(pl.multiple_of(base + which * half, LANE), half)

    def rows(block):
        return pl.ds(pl.multiple_of(block * tok, tok), tok)

    def y_send(k, o):
        own, scr = chunks[k][0], chunks[k][1]
        to = 2 * lax.rem(y + o, n_y) + c
        return rcopy(
            own.at[:, cols(k, p)], scr.at[rows(d), cols(k, p)],
            ys.at[o - 1, k], yr.at[o - 1, k], (v, to),
        )

    def came(o):
        return lax.rem(y + n_y - o, n_y)

    def fwd(k, o, which, block, send, recv, dev):
        scr = chunks[k][1]
        ref = scr.at[rows(block), cols(k, which)]
        return rcopy(ref, ref, send.at[o - 1, k], recv.at[o - 1, k], dev)

    def x_fwd(k, o, which):
        return fwd(k, o, which, 2 * came(o) + c, xs, xr, (v_pair, d))

    def d1_fwd(k, o, side):
        return fwd(k, o, p, 2 * came(o) + side, d1s, d1r, (v, mate))

    def d2_fwd(k, o, side):
        return fwd(k, o, 1 - p, 2 * came(o) + side, d2s, d2r, (v, mate))

    sends = []
    mate_copies = [
        rcopy(th_own, th.at[own_rows], pc_s.at[0], pc_r.at[0], (v, mate)),
        rcopy(sh_own, sh.at[own_rows], pc_s.at[1], pc_r.at[1], (v, mate)),
    ]
    for k in range(n_ch):
        for o in range(1, n_y):
            cp = y_send(k, o)
            cp.start()
            sends.append(cp)
        if k == 0:
            for cp in mate_copies:
                cp.start()
    loss_copies = []
    for dd in range(1, n_dp):
        cp = rcopy(
            loss, lsc.at[d], ls_s.at[dd - 1], ls_r.at[dd - 1], (v, lax.rem(d + dd, n_dp))
        )
        cp.start()
        loss_copies.append(cp)
    lsc[d] = loss[...]

    def product(k, chip, first):
        own, scr, tab, acc, base, width = chunks[k]
        two = pl.ds(pl.multiple_of(chip * 2 * tok, 2 * tok), 2 * tok)
        part = dot_t(tab[:, pl.ds(base, width)], scr[two, pl.ds(base, width)])
        if first:
            acc[:, two] = part
        else:
            acc[:, two] += part

    def prepare(k):
        own, scr, tab, acc, base, width = chunks[k]
        loads[k].wait()
        if tab is table:
            @pl.loop(0, table.shape[0] // 64)
            def _(r):
                rsl = pl.ds(pl.multiple_of(r * 64, 64), 64)
                sc = scales[rsl, :]
                for g in range(width // GROUP):
                    lane = pl.ds(base + g * GROUP, GROUP)
                    col = (base + g * GROUP) // GROUP
                    wide = table[rsl, lane].astype(jnp.float32) * sc[:, col : col + 1]
                    table[rsl, lane] = wide.astype(jnp.bfloat16)
        else:
            for b in range(base, base + width, 256):
                wgt_t[pl.ds(b, 256), :] = wgt[:, pl.ds(b, 256)].T

    for cp in own_loads:
        cp.wait()
    firsts = [k == 0 or chunks[k][3] is not chunks[k - 1][3] for k in range(n_ch)]
    for k in range(n_ch + 2):
        if k < n_ch:
            prepare(k)
            for o in range(1, n_y):
                fwd(
                    k, o, p, 2 * came(o) + c, ys, yr, (v, mate)
                ).wait_recv()
                for cp in (x_fwd(k, o, p), d1_fwd(k, o, c)):
                    cp.start()
                    sends.append(cp)
        if 1 <= k <= n_ch:
            for o in range(1, n_y):
                x_fwd(k - 1, o, 1 - p).wait_recv()
                cp = d2_fwd(k - 1, o, c)
                cp.start()
                sends.append(cp)
        if k < n_ch:
            if k == 0:
                for which, (own, scr) in enumerate(((th_own, th), (sh_own, sh))):
                    land = scr.at[rows(mate)]
                    rcopy(own, land, pc_s.at[which], pc_r.at[which], (v, mate)).wait_recv()
            product(k, y, firsts[k])
        if k >= 2:
            for o in range(1, n_y):
                fwd(
                    k - 2, o, p, 2 * came(o) + 1 - c, d1s, d1r, (v, mate)
                ).wait_recv()
                fwd(
                    k - 2, o, 1 - p, 2 * came(o) + 1 - c, d2s, d2r, (v, mate)
                ).wait_recv()
            if n_y > 1:
                @pl.loop(1, n_y)
                def _(o):
                    product(k - 2, lax.rem(y + n_y - o, n_y), firsts[k - 2])

    n_tok = n_dp * tok

    @pl.loop(0, n_dp)
    def _(j):
        sl = pl.ds(pl.multiple_of(j * tok, tok), tok)
        t_max = jnp.max(tlog[:, sl], axis=0, keepdims=True)
        s_max = jnp.max(slog[:, sl], axis=0, keepdims=True)
        te = jnp.exp(tlog[:, sl] - t_max)
        t_sum = jnp.sum(te, axis=0, keepdims=True)
        x_sum = jnp.sum(te * (tlog[:, sl] - slog[:, sl]), axis=0, keepdims=True)
        tlog[:, sl] = te
        se = jnp.exp(slog[:, sl] - s_max)
        s_sum = jnp.sum(se, axis=0, keepdims=True)
        slog[:, sl] = se
        stat[:, sl] = jnp.concatenate(
            [t_max, t_sum, x_sum, s_max, s_sum, jnp.zeros((3, tok), jnp.float32)], axis=0
        )

    def merge(parts):
        t_top = functools.reduce(jnp.maximum, [x[0:1] for x in parts])
        s_top = functools.reduce(jnp.maximum, [x[3:4] for x in parts])
        t_sum = x_sum = s_sum = 0.0
        for x in parts:
            t_w = jnp.exp(x[0:1] - t_top)
            t_sum += x[1:2] * t_w
            x_sum += x[2:3] * t_w
            s_sum += x[4:5] * jnp.exp(x[3:4] - s_top)
        return t_top, t_sum, x_sum, s_top, s_sum

    for i, peer in enumerate(peers_a):
        cp = rcopy(stat, in_a.at[i], a_s.at[i], a_r.at[i], peer)
        cp.start()
        sends.append(cp)
    for i, peer in enumerate(peers_a):
        rcopy(stat, in_a.at[i], a_s.at[i], a_r.at[i], peer).wait_recv()
    stat_b[...] = jnp.concatenate(
        list(merge([stat[...]] + [in_a[i] for i in range(len(peers_a))]))
        + [jnp.zeros((3, n_tok), jnp.float32)], axis=0
    )
    for i, peer in enumerate(peers_b):
        cp = rcopy(stat_b, in_b.at[i], b_s.at[i], b_r.at[i], peer)
        cp.start()
        sends.append(cp)
    for dd in range(1, n_dp):
        other = lax.rem(d + n_dp - dd, n_dp)
        rcopy(loss, lsc.at[other], ls_s.at[dd - 1], ls_r.at[dd - 1], (v, mate)).wait_recv()
    for i, peer in enumerate(peers_b):
        rcopy(stat_b, in_b.at[i], b_s.at[i], b_r.at[i], peer).wait_recv()
    t_top, t_sum, x_sum, s_top, s_sum = merge(
        [stat_b[...]] + [in_b[i] for i in range(len(peers_b))]
    )
    t_lse = t_top + jnp.log(t_sum)
    s_lse = s_top + jnp.log(s_sum)
    fin[...] = jnp.concatenate(
        [
            x_sum / t_sum - t_lse + s_lse,
            jnp.exp(stat[0:1] - t_lse),
            jnp.exp(stat[3:4] - s_lse),
            jnp.zeros((5, n_tok), jnp.float32),
        ],
        axis=0,
    )
    kl_out[...] = fin[0:1, own_rows]

    @pl.loop(0, n_dp)
    def _(j):
        sl = pl.ds(pl.multiple_of(j * tok, tok), tok)
        f = fin[:, sl]
        grad[:, sl] = (
            lsc[j][0:1] * (slog[:, sl] * f[2:3] - tlog[:, sl] * f[1:2])
        ).astype(jnp.bfloat16)

    order = []
    for i in range(n_z1):
        order += [i, n_z1 + i]
    order += [i for i in range(n_z) if i not in order]

    def hidden_part(z):
        for pp in range(2):
            feat = wgt_t[pl.ds((2 * z + pp) * rv, rv), :]
            for yy in range(n_y):
                part = jnp.dot(
                    feat, grad[:, pl.ds(yy * 2 * tok, 2 * tok)],
                    preferred_element_type=jnp.float32,
                )
                left, right = part[:, :tok], part[:, tok:]
                mine[z, pp, yy] = jnp.where(c == 0, left, right)
                theirs[z, pp, yy] = jnp.where(c == 0, right, left).astype(jnp.bfloat16)

    def core_copy(z):
        return rcopy(theirs.at[z], core_in.at[z], cs.at[z], cr.at[z], (v, mate))

    def launch(cp):
        cp.start()
        sends.append(cp)

    def y1_copy(z, o):
        to = 2 * lax.rem(y + o, n_y) + c
        return rcopy(
            y1s.at[z, o - 1], y1r.at[z, o - 1], r1s.at[z, o - 1], r1r.at[z, o - 1], (v, to)
        )

    def x1_copy(z):
        return rcopy(x1s.at[z], x1r.at[z], r2s.at[z, 0], r2r.at[z, 0], (v_pair, d))

    def x2_copy(z):
        return rcopy(
            x2s.at[z - n_z1], x2r.at[z - n_z1], r1s.at[z, 0], r1r.at[z, 0], (v_pair, d)
        )

    def y2_copy(z, o):
        to = 2 * lax.rem(y + o, n_y) + c
        return rcopy(
            y2s.at[z - n_z1, o - 1], y2r.at[z - n_z1, o - 1],
            r2s.at[z, o - 1], r2r.at[z, o - 1], (v, to),
        )

    def after_core(z):
        core_copy(z).wait_recv()
        if z < n_z1:
            for o in range(1, n_y):
                to = lax.rem(y + o, n_y)
                for pp in range(2):
                    y1s[z, o - 1, pp] = (
                        mine[z, pp, to] + core_in[z, pp, to].astype(jnp.float32)
                    ).astype(jnp.bfloat16)
                launch(y1_copy(z, o))
        else:
            for yy in range(n_y):
                x2s[z - n_z1, yy] = (
                    mine[z, 1 - p, yy] + core_in[z, 1 - p, yy].astype(jnp.float32)
                ).astype(jnp.bfloat16)
            launch(x2_copy(z))

    def after_first(z):
        if z < n_z1:
            for o in range(1, n_y):
                y1_copy(z, o).wait_recv()

            def total(which):
                out = mine[z, which, y] + core_in[z, which, y].astype(jnp.float32)
                for o in range(1, n_y):
                    out += y1r[z, o - 1, which].astype(jnp.float32)
                return out

            x1s[z] = total(1 - p).astype(jnp.bfloat16)
            launch(x1_copy(z))
            zf[z] = total(p)
        else:
            x2_copy(z).wait_recv()

            def total(yy):
                return (
                    mine[z, p, yy] + core_in[z, p, yy].astype(jnp.float32)
                    + x2r[z - n_z1, yy].astype(jnp.float32)
                )

            for o in range(1, n_y):
                y2s[z - n_z1, o - 1] = total(lax.rem(y + o, n_y)).astype(jnp.bfloat16)
                launch(y2_copy(z, o))
            zf[z] = total(y)

    def z_copy(z):
        return rcopy(zs.at[z], zr.at[q], z_ss.at[z], z_rs.at[q], (2 * z + p, d))

    def after_second(z):
        if z < n_z1:
            x1_copy(z).wait_recv()
            full = zf[z] + x1r[z].astype(jnp.float32)
        else:
            full = zf[z]
            for o in range(1, n_y):
                y2_copy(z, o).wait_recv()
                full += y2r[z - n_z1, o - 1].astype(jnp.float32)
        zf[z] = full
        zs[z] = full.astype(jnp.bfloat16)

        @pl.when(q != z)
        def _():
            z_copy(z).start()

    n_gw = sh.shape[1] // 512
    gw_copies = []

    def weight_part(b):
        sl = pl.ds(b * 512, 512)
        gw_buf[:, sl] = jnp.dot(
            grad[...], sh[:, sl], preferred_element_type=jnp.float32
        ).astype(jnp.bfloat16)
        cp = pltpu.make_async_copy(gw_buf.at[:, sl], gw_out.at[:, sl], gw_sem.at[b])
        cp.start()
        gw_copies.append(cp)

    for z in order:
        hidden_part(z)
        launch(core_copy(z))
    for z in order:
        after_core(z)
    for b in range(n_gw):
        weight_part(b)
    for z in order:
        after_first(z)
    for z in order:
        after_second(z)
    zf_q = zf[q]
    mine_sum = [zf_q]
    total = zf_q
    for o in range(1, n_z):
        src = lax.rem(q + o, n_z)
        rcopy(zs.at[src], zr.at[src], z_ss.at[src], z_rs.at[src], (v_pair, d)).wait_recv()
        total += zr[src].astype(jnp.float32)
    gh_out[...] = total.T.astype(jnp.bfloat16)

    for cp in sends + loss_copies + mate_copies:
        cp.wait_send()
    for o in range(1, n_z):
        dst = lax.rem(q + o, n_z)
        rcopy(zs.at[dst], zr.at[q], z_ss.at[dst], z_rs.at[q], (2 * dst + p, d)).wait_send()
    for cp in gw_copies:
        cp.wait()


def solution(mesh):
    n_vocab, n_dp = mesh.shape["vocab"], mesh.shape["dp"]

    def local(th_own, sh_own, codes, scales, weight, loss_scale):
        tok, dt = th_own.shape
        ds_ = sh_own.shape[1]
        rows = codes.shape[0]
        n_tok = tok * n_dp
        n_y, n_z = n_dp // 2, n_vocab // 2
        n_off, n_z1 = n_y - 1, n_z // 2
        n_z2 = n_z - n_z1
        rv = ds_ // n_vocab
        n_ch = dt // step_width(dt) + ds_ // step_width(ds_)
        n_a, n_b = 2 * n_dp - 1, n_z - 1
        bf, f32 = jnp.bfloat16, jnp.float32
        V, D = pltpu.VMEM, pltpu.SemaphoreType.DMA
        loss = jnp.broadcast_to(loss_scale.astype(f32)[None, :], (8, tok))
        any_spec = pl.BlockSpec(memory_space=pl.ANY)
        vm_spec = pl.BlockSpec(memory_space=pltpu.VMEM)
        kl, gh, gw = pl.pallas_call(
            functools.partial(kernel, n_vocab, n_dp),
            out_shape=(
                jax.ShapeDtypeStruct((1, tok), f32),
                jax.ShapeDtypeStruct((tok, rv), bf),
                jax.ShapeDtypeStruct((rows, ds_), bf),
            ),
            in_specs=[any_spec, any_spec, any_spec, vm_spec, any_spec, vm_spec],
            out_specs=(vm_spec, vm_spec, any_spec),
            scratch_shapes=[
                V((n_tok, dt), bf), V((n_tok, ds_), bf), V((rows, dt), bf), V((rows, ds_), bf),
                V((ds_, rows), bf), V((rows, n_tok), f32), V((rows, n_tok), f32),
                V((n_dp, 8, tok), f32), V((8, n_tok), f32), V((8, n_tok), f32),
                V((8, n_tok), f32), V((n_a, 8, n_tok), f32), V((n_b, 8, n_tok), f32),
                V((rows, n_tok), bf), V((rows, ds_), bf),
                V((n_z, 2, n_y, rv, tok), f32), V((n_z, 2, n_y, rv, tok), bf),
                V((n_z, 2, n_y, rv, tok), bf),
                V((n_z1, n_off, 2, rv, tok), bf), V((n_z1, n_off, 2, rv, tok), bf),
                V((n_z1, rv, tok), bf), V((n_z1, rv, tok), bf),
                V((n_z2, n_y, rv, tok), bf), V((n_z2, n_y, rv, tok), bf),
                V((n_z2, n_off, rv, tok), bf), V((n_z2, n_off, rv, tok), bf),
                V((n_z, rv, tok), bf), V((n_z, rv, tok), bf), V((n_z, rv, tok), f32),
                D((n_ch + 2,)), D((ds_ // 512,)), D((2,)), D((2,)),
                *[D((n_off, n_ch))] * 8,
                D((n_dp - 1,)), D((n_dp - 1,)), D((n_a,)), D((n_a,)), D((n_b,)), D((n_b,)),
                D((n_z,)), D((n_z,)), *[D((n_z, n_off))] * 4, D((n_z,)), D((n_z,)),
            ],
            compiler_params=pltpu.CompilerParams(
                collective_id=0, has_side_effects=True, vmem_limit_bytes=60 * 1024 * 1024
            ),
            name="distill",
        )(th_own, sh_own, codes, scales, weight, loss)
        return kl.reshape(tok), gh, gw

    in_specs = (
        P("dp", None),
        P("dp", None),
        P(("vocab", "dp"), None),
        P(("vocab", "dp"), None),
        P(("vocab", "dp"), None),
        P("dp"),
    )
    out_specs = (P("dp"), P("dp", "vocab"), P(("vocab", "dp"), None))
    return jax.shard_map(local, mesh=mesh, in_specs=in_specs, out_specs=out_specs, check_vma=False)
```

```python
import functools

import jax
import jax.numpy as jnp
from jax import lax
from jax.experimental import pallas as pl
from jax.experimental.pallas import tpu as pltpu
from jax.sharding import PartitionSpec as P

GROUP = 128
LANE = 128
MESH = pl.DeviceIdType.MESH


def step_width(cols):
    units = cols // 256
    per = max(k for k in (1, 2, 3) if units % k == 0)
    return per * 256


def dot_t(left_rows, right_rows):
    return lax.dot_general(
        left_rows, right_rows, (((1,), (1,)), ((), ())), preferred_element_type=jnp.float32
    )


def kernel(
    n_vocab, n_dp,
    th_own, sh_own, codes, scales, weight, loss_in,
    kl_out, gh_out, gw_out,
    th, sh, table, wgt, wgt_t, tlog, slog, lsc, stat, stat_b, fin, in_a, in_b,
    grad, gw_buf, mine, theirs, core_in,
    y1s, y1r, x1s, x1r, x2s, x2r, y2s, y2r, zs, zr, zf,
    sc_rows, loss_row, ld_sem, gw_sem, pc_s, pc_r, hop_s, hop_r,
    ls_s, ls_r, a_s, a_r, b_s, b_r, cs, cr, r1s, r1r, r2s, r2r, z_ss, z_rs,
):
    v, d = lax.axis_index("vocab"), lax.axis_index("dp")
    c, y = lax.rem(d, 2), lax.div(d, 2)
    p, q = lax.rem(v, 2), lax.div(v, 2)
    n_y, n_z = n_dp // 2, n_vocab // 2
    n_off = n_y - 1
    mate = 2 * y + 1 - c
    v_pair = 2 * q + 1 - p
    r = lax.rem(q, 2)
    v_quad = 2 * (q + 1 - 2 * r) + p
    tok = th_own.shape[0]
    rv = zr.shape[1]
    n_z1 = n_z // 2

    def rcopy(src, dst, send, recv, dev):
        return pltpu.make_async_remote_copy(
            src_ref=src, dst_ref=dst, send_sem=send, recv_sem=recv,
            device_id=dev, device_id_type=MESH,
        )

    chunks = []
    for own, scr, tab, acc in ((th_own, th, table, tlog), (sh_own, sh, wgt, slog)):
        width = step_width(own.shape[1])
        for base in range(0, own.shape[1], width):
            chunks.append((own, scr, tab, acc, base, width))
    n_ch = len(chunks)

    loads = []
    for k, (own, scr, tab, acc, base, width) in enumerate(chunks):
        src = codes if tab is table else weight
        cp = pltpu.make_async_copy(
            src.at[:, pl.ds(base, width)], tab.at[:, pl.ds(base, width)], ld_sem.at[k]
        )
        cp.start()
        loads.append(cp)
    own_rows = pl.ds(pl.multiple_of(d * tok, tok), tok)
    own_loads = [
        pltpu.make_async_copy(th_own, th.at[own_rows], ld_sem.at[n_ch]),
        pltpu.make_async_copy(sh_own, sh.at[own_rows], ld_sem.at[n_ch + 1]),
    ]
    for cp in own_loads:
        cp.start()

    peers_a = []
    for dv in range(2):
        for dd in range(n_dp):
            if dv or dd:
                peers_a.append((v if dv == 0 else v_pair, lax.rem(d + dd, n_dp)))
    from_a = []
    peers_b = [(2 * lax.rem(q + o, n_z) + p, d) for o in range(1, n_z)]
    barrier = pltpu.get_barrier_semaphore()
    for peer in peers_a + peers_b:
        pl.semaphore_signal(barrier, inc=1, device_id=peer, device_id_type=MESH)
    pl.semaphore_wait(barrier, len(peers_a) + len(peers_b))

    quarter = tok // 4

    def rows(block):
        return pl.ds(pl.multiple_of(block * tok, tok), tok)

    def region(k, block, piece, half=None):
        scr, base, width = chunks[k][1], chunks[k][4], chunks[k][5]
        first, size = block * tok + piece * quarter, quarter
        if half is not None:
            size = quarter // 2
            first += half * size
        return scr.at[pl.ds(pl.multiple_of(first, size), size), pl.ds(base, width)]

    A, B, C, E = 2 * r + p, 2 * r + 1 - p, 2 * (1 - r) + p, 2 * (1 - r) + 1 - p
    X, Z = (v_pair, d), (v_quad, d)
    Y_A, Y_E, X_A, Z_A, X_C, Z_B, D_A, D_B, D_C, D_E = range(10)

    def far_by_y(k):
        return k % 3 == 2

    def came(o):
        return lax.rem(y + n_y - o, n_y)

    def y_send(k, o, kind):
        own, base, width = chunks[k][0], chunks[k][4], chunks[k][5]
        piece = A if kind == Y_A else E
        src = own.at[pl.ds(pl.multiple_of(piece * quarter, quarter), quarter), pl.ds(base, width)]
        to = 2 * lax.rem(y + o, n_y) + c
        return rcopy(
            src, region(k, d, piece), hop_s.at[kind, o - 1, k], hop_r.at[kind, o - 1, k], (v, to)
        )

    def hop(kind, k, o, side, piece, dev, half=None):
        ref = region(k, 2 * came(o) + side, piece, half)
        return rcopy(ref, ref, hop_s.at[kind, o - 1, k], hop_r.at[kind, o - 1, k], dev)

    def to_mate(kind, k, o, piece):
        launch(hop(kind, k, o, c, piece, (v, mate)))

    def launch(cp):
        cp.start()
        sends.append(cp)

    def stage_y(k):
        for o in range(1, n_y):
            hop(Y_A, k, o, c, A, X).wait_recv()
            launch(hop(X_A, k, o, c, A, X))
            launch(hop(Z_A, k, o, c, A, Z))
            to_mate(D_A, k, o, A)

    def stage_xz(k):
        for o in range(1, n_y):
            hop(X_A, k, o, c, B, X).wait_recv()
            if not far_by_y(k):
                launch(hop(Z_B, k, o, c, B, Z, 1))
            to_mate(D_B, k, o, B)
            hop(Z_A, k, o, c, C, Z).wait_recv()
            if not far_by_y(k):
                launch(hop(X_C, k, o, c, C, X, 0))
            to_mate(D_C, k, o, C)

    def stage_far(k):
        for o in range(1, n_y):
            if far_by_y(k):
                hop(Y_E, k, o, c, E, X).wait_recv()
            else:
                hop(X_C, k, o, c, E, X, 0).wait_recv()
                hop(Z_B, k, o, c, E, Z, 1).wait_recv()
            to_mate(D_E, k, o, E)

    def stage_mate(k):
        for o in range(1, n_y):
            for kind, piece in ((D_A, A), (D_B, B), (D_C, C), (D_E, E)):
                hop(kind, k, o, 1 - c, piece, X).wait_recv()

    sends = []
    mate_copies = [
        rcopy(th_own, th.at[own_rows], pc_s.at[0], pc_r.at[0], (v, mate)),
        rcopy(sh_own, sh.at[own_rows], pc_s.at[1], pc_r.at[1], (v, mate)),
    ]
    for k in range(n_ch):
        for o in range(1, n_y):
            launch(y_send(k, o, Y_A))
            if far_by_y(k):
                launch(y_send(k, o, Y_E))
        if k == 0:
            for cp in mate_copies:
                cp.start()
    loss_copies = []
    loss_row[...] = jnp.broadcast_to(
        loss_in[...].astype(jnp.float32).reshape(1, tok), loss_row.shape
    )
    lsc[d] = loss_row[...]
    groups = scales.shape[0]
    pad = jnp.zeros((sc_rows.shape[1] - groups, LANE), jnp.float32)
    for b in range(0, scales.shape[1], LANE):
        sc_rows[pl.ds(b, LANE), :] = jnp.concatenate(
            [scales[:, pl.ds(b, LANE)], pad], axis=0
        ).T

    def product(k, chip, first):
        own, scr, tab, acc, base, width = chunks[k]
        two = pl.ds(pl.multiple_of(chip * 2 * tok, 2 * tok), 2 * tok)
        part = dot_t(tab[:, pl.ds(base, width)], scr[two, pl.ds(base, width)])
        if first:
            acc[:, two] = part
        else:
            acc[:, two] += part

    def prepare(k):
        own, scr, tab, acc, base, width = chunks[k]
        loads[k].wait()
        if tab is table:
            @pl.loop(0, table.shape[0] // 64)
            def _(i):
                rsl = pl.ds(pl.multiple_of(i * 64, 64), 64)
                sc = sc_rows[rsl, :]
                for g in range(width // GROUP):
                    lane = pl.ds(base + g * GROUP, GROUP)
                    col = (base + g * GROUP) // GROUP
                    wide = table[rsl, lane].astype(jnp.float32) * sc[:, col : col + 1]
                    table[rsl, lane] = wide.astype(jnp.bfloat16)

    for cp in own_loads:
        cp.wait()
    firsts = [k == 0 or chunks[k][3] is not chunks[k - 1][3] for k in range(n_ch)]
    lag = 3
    for k in range(n_ch + lag):
        if k < n_ch:
            prepare(k)
            stage_y(k)
        if 1 <= k <= n_ch:
            stage_xz(k - 1)
        if 2 <= k <= n_ch + 1:
            stage_far(k - 2)
        if k < n_ch:
            if k == 0:
                for which, (own, scr) in enumerate(((th_own, th), (sh_own, sh))):
                    land = scr.at[rows(mate)]
                    rcopy(own, land, pc_s.at[which], pc_r.at[which], (v, mate)).wait_recv()
            product(k, y, firsts[k])
        if k >= lag:
            stage_mate(k - lag)
            if n_y > 1:
                @pl.loop(1, n_y)
                def _(o):
                    product(k - lag, lax.rem(y + n_y - o, n_y), firsts[k - lag])
        if k == n_ch - 1:
            for dd in range(1, n_dp):
                cp = rcopy(
                    loss_row, lsc.at[d], ls_s.at[dd - 1], ls_r.at[dd - 1],
                    (v, lax.rem(d + dd, n_dp)),
                )
                cp.start()
                loss_copies.append(cp)

    n_tok = n_dp * tok

    @pl.loop(0, n_dp)
    def _(j):
        sl = pl.ds(pl.multiple_of(j * tok, tok), tok)
        t_max = jnp.max(tlog[:, sl], axis=0, keepdims=True)
        s_max = jnp.max(slog[:, sl], axis=0, keepdims=True)
        te = jnp.exp(tlog[:, sl] - t_max)
        t_sum = jnp.sum(te, axis=0, keepdims=True)
        x_sum = jnp.sum(te * (tlog[:, sl] - slog[:, sl]), axis=0, keepdims=True)
        tlog[:, sl] = te
        se = jnp.exp(slog[:, sl] - s_max)
        s_sum = jnp.sum(se, axis=0, keepdims=True)
        slog[:, sl] = se
        stat[:, sl] = jnp.concatenate(
            [t_max, t_sum, x_sum, s_max, s_sum, jnp.zeros((3, tok), jnp.float32)], axis=0
        )

    def merge(parts):
        t_top = functools.reduce(jnp.maximum, [x[0:1] for x in parts])
        s_top = functools.reduce(jnp.maximum, [x[3:4] for x in parts])
        t_sum = x_sum = s_sum = 0.0
        for x in parts:
            t_w = jnp.exp(x[0:1] - t_top)
            t_sum += x[1:2] * t_w
            x_sum += x[2:3] * t_w
            s_sum += x[4:5] * jnp.exp(x[3:4] - s_top)
        return t_top, t_sum, x_sum, s_top, s_sum

    for i, peer in enumerate(peers_a):
        cp = rcopy(stat, in_a.at[i], a_s.at[i], a_r.at[i], peer)
        cp.start()
        sends.append(cp)
    for b in range(0, wgt.shape[1], 256):
        wgt_t[pl.ds(b, 256), :] = wgt[:, pl.ds(b, 256)].T
    for i, peer in enumerate(peers_a):
        rcopy(stat, in_a.at[i], a_s.at[i], a_r.at[i], peer).wait_recv()
    stat_b[...] = jnp.concatenate(
        list(merge([stat[...]] + [in_a[i] for i in range(len(peers_a))]))
        + [jnp.zeros((3, n_tok), jnp.float32)], axis=0
    )
    for i, peer in enumerate(peers_b):
        cp = rcopy(stat_b, in_b.at[i], b_s.at[i], b_r.at[i], peer)
        cp.start()
        sends.append(cp)
    for dd in range(1, n_dp):
        other = lax.rem(d + n_dp - dd, n_dp)
        rcopy(loss_row, lsc.at[other], ls_s.at[dd - 1], ls_r.at[dd - 1], (v, mate)).wait_recv()
    for i, peer in enumerate(peers_b):
        rcopy(stat_b, in_b.at[i], b_s.at[i], b_r.at[i], peer).wait_recv()
    t_top, t_sum, x_sum, s_top, s_sum = merge(
        [stat_b[...]] + [in_b[i] for i in range(len(peers_b))]
    )
    t_lse = t_top + jnp.log(t_sum)
    s_lse = s_top + jnp.log(s_sum)
    fin[...] = jnp.concatenate(
        [
            x_sum / t_sum - t_lse + s_lse,
            jnp.exp(stat[0:1] - t_lse),
            jnp.exp(stat[3:4] - s_lse),
            jnp.zeros((5, n_tok), jnp.float32),
        ],
        axis=0,
    )
    kl_out[...] = fin[0:1, own_rows]

    @pl.loop(0, n_dp)
    def _(j):
        sl = pl.ds(pl.multiple_of(j * tok, tok), tok)
        f = fin[:, sl]
        grad[:, sl] = (
            lsc[j][0:1] * (slog[:, sl] * f[2:3] - tlog[:, sl] * f[1:2])
        ).astype(jnp.bfloat16)

    order = []
    for i in range(n_z1):
        order += [i, n_z1 + i]
    order += [i for i in range(n_z) if i not in order]

    def hidden_part(z):
        for pp in range(2):
            feat = wgt_t[pl.ds((2 * z + pp) * rv, rv), :]
            for yy in range(n_y):
                part = jnp.dot(
                    feat, grad[:, pl.ds(yy * 2 * tok, 2 * tok)],
                    preferred_element_type=jnp.float32,
                )
                left, right = part[:, :tok], part[:, tok:]
                mine[z, pp, yy] = jnp.where(c == 0, left, right)
                theirs[z, pp, yy] = jnp.where(c == 0, right, left).astype(jnp.bfloat16)

    def core_copy(z):
        return rcopy(theirs.at[z], core_in.at[z], cs.at[z], cr.at[z], (v, mate))

    def y1_copy(z, o):
        to = 2 * lax.rem(y + o, n_y) + c
        return rcopy(
            y1s.at[z, o - 1], y1r.at[z, o - 1], r1s.at[z, o - 1], r1r.at[z, o - 1], (v, to)
        )

    def x1_copy(z):
        return rcopy(x1s.at[z], x1r.at[z], r2s.at[z, 0], r2r.at[z, 0], (v_pair, d))

    def x2_copy(z):
        return rcopy(
            x2s.at[z - n_z1], x2r.at[z - n_z1], r1s.at[z, 0], r1r.at[z, 0], (v_pair, d)
        )

    def y2_copy(z, o):
        to = 2 * lax.rem(y + o, n_y) + c
        return rcopy(
            y2s.at[z - n_z1, o - 1], y2r.at[z - n_z1, o - 1],
            r2s.at[z, o - 1], r2r.at[z, o - 1], (v, to),
        )

    def after_core(z):
        core_copy(z).wait_recv()
        if z < n_z1:
            for o in range(1, n_y):
                to = lax.rem(y + o, n_y)
                for pp in range(2):
                    y1s[z, o - 1, pp] = (
                        mine[z, pp, to] + core_in[z, pp, to].astype(jnp.float32)
                    ).astype(jnp.bfloat16)
                launch(y1_copy(z, o))
        else:
            for yy in range(n_y):
                x2s[z - n_z1, yy] = (
                    mine[z, 1 - p, yy] + core_in[z, 1 - p, yy].astype(jnp.float32)
                ).astype(jnp.bfloat16)
            launch(x2_copy(z))

    def after_first(z):
        if z < n_z1:
            for o in range(1, n_y):
                y1_copy(z, o).wait_recv()

            def total(which):
                out = mine[z, which, y] + core_in[z, which, y].astype(jnp.float32)
                for o in range(1, n_y):
                    out += y1r[z, o - 1, which].astype(jnp.float32)
                return out

            x1s[z] = total(1 - p).astype(jnp.bfloat16)
            launch(x1_copy(z))
            zf[z] = total(p)
        else:
            x2_copy(z).wait_recv()

            def total(yy):
                return (
                    mine[z, p, yy] + core_in[z, p, yy].astype(jnp.float32)
                    + x2r[z - n_z1, yy].astype(jnp.float32)
                )

            for o in range(1, n_y):
                y2s[z - n_z1, o - 1] = total(lax.rem(y + o, n_y)).astype(jnp.bfloat16)
                launch(y2_copy(z, o))
            zf[z] = total(y)

    def z_copy(z):
        return rcopy(zs.at[z], zr.at[q], z_ss.at[z], z_rs.at[q], (2 * z + p, d))

    def after_second(z):
        if z < n_z1:
            x1_copy(z).wait_recv()
            full = zf[z] + x1r[z].astype(jnp.float32)
        else:
            full = zf[z]
            for o in range(1, n_y):
                y2_copy(z, o).wait_recv()
                full += y2r[z - n_z1, o - 1].astype(jnp.float32)
        zf[z] = full
        zs[z] = full.astype(jnp.bfloat16)

        @pl.when(q != z)
        def _():
            z_copy(z).start()

    n_gw = sh.shape[1] // 512
    gw_copies = []

    def weight_part(b):
        sl = pl.ds(b * 512, 512)
        gw_buf[:, sl] = jnp.dot(
            grad[...], sh[:, sl], preferred_element_type=jnp.float32
        ).astype(jnp.bfloat16)
        cp = pltpu.make_async_copy(gw_buf.at[:, sl], gw_out.at[:, sl], gw_sem.at[b])
        cp.start()
        gw_copies.append(cp)

    for z in order:
        hidden_part(z)
        launch(core_copy(z))
    for z in order:
        after_core(z)
    for b in range(n_gw):
        weight_part(b)
    for z in order:
        after_first(z)
    for z in order:
        after_second(z)
    zf_q = zf[q]
    mine_sum = [zf_q]
    total = zf_q
    for o in range(1, n_z):
        src = lax.rem(q + o, n_z)
        rcopy(zs.at[src], zr.at[src], z_ss.at[src], z_rs.at[src], (v_pair, d)).wait_recv()
        total += zr[src].astype(jnp.float32)
    gh_out[...] = total.astype(jnp.bfloat16)

    for cp in sends + loss_copies + mate_copies:
        cp.wait_send()
    for o in range(1, n_z):
        dst = lax.rem(q + o, n_z)
        rcopy(zs.at[dst], zr.at[q], z_ss.at[dst], z_rs.at[q], (2 * dst + p, d)).wait_send()
    for cp in gw_copies:
        cp.wait()


def hand_over(kl, gh, gw):
    parts = 4
    step = gw.shape[0] // parts

    def move(kl_in, gh_in, gw_in, kl_to, gh_to, gw_to, kl_v, gh_v, gw_v, sem_in, sem_out):
        plan = [(kl_in, kl_v, kl_to), (gh_in, gh_v, gh_to)]
        for i in range(parts):
            sl = pl.ds(i * step, step)
            plan.append((gw_in.at[sl], gw_v.at[sl], gw_to.at[sl]))
        reads = [pltpu.make_async_copy(a, b, sem_in.at[i]) for i, (a, b, _) in enumerate(plan)]
        writes = [pltpu.make_async_copy(b, e, sem_out.at[i]) for i, (_, b, e) in enumerate(plan)]
        for cp in reads:
            cp.start()
        for cp, out in zip(reads, writes):
            cp.wait()
            out.start()
        for out in writes:
            out.wait()

    spec = pl.BlockSpec(memory_space=pl.ANY)
    arrays = (kl, gh, gw)
    return pl.pallas_call(
        move,
        out_shape=tuple(jax.ShapeDtypeStruct(a.shape, a.dtype) for a in arrays),
        in_specs=[spec] * 3,
        out_specs=(spec,) * 3,
        scratch_shapes=[pltpu.VMEM(a.shape, a.dtype) for a in arrays]
        + [pltpu.SemaphoreType.DMA((parts + 2,))] * 2,
        name="hand_over",
    )(*arrays)


def solution(mesh):
    n_vocab, n_dp = mesh.shape["vocab"], mesh.shape["dp"]

    def local(th_own, sh_own, codes, scales, weight, loss_scale):
        tok, dt = th_own.shape
        ds_ = sh_own.shape[1]
        rows = codes.shape[0]
        n_tok = tok * n_dp
        n_y, n_z = n_dp // 2, n_vocab // 2
        n_off, n_z1 = n_y - 1, n_z // 2
        n_z2 = n_z - n_z1
        rv = ds_ // n_vocab
        n_ch = dt // step_width(dt) + ds_ // step_width(ds_)
        n_a, n_b = 2 * n_dp - 1, n_z - 1
        bf, f32 = jnp.bfloat16, jnp.float32
        V, D = pltpu.VMEM, pltpu.SemaphoreType.DMA
        any_spec = pl.BlockSpec(memory_space=pl.ANY)
        vm_spec = pl.BlockSpec(memory_space=pltpu.VMEM)
        kl, gh, gw = pl.pallas_call(
            functools.partial(kernel, n_vocab, n_dp),
            out_shape=(
                jax.ShapeDtypeStruct((1, tok), f32),
                jax.ShapeDtypeStruct((rv, tok), bf),
                jax.ShapeDtypeStruct((rows, ds_), bf),
            ),
            in_specs=[any_spec, any_spec, any_spec, vm_spec, any_spec, vm_spec],
            out_specs=(vm_spec, vm_spec, any_spec),
            scratch_shapes=[
                V((n_tok, dt), bf), V((n_tok, ds_), bf), V((rows, dt), bf), V((rows, ds_), bf),
                V((ds_, rows), bf), V((rows, n_tok), f32), V((rows, n_tok), f32),
                V((n_dp, 8, tok), f32), V((8, n_tok), f32), V((8, n_tok), f32),
                V((8, n_tok), f32), V((n_a, 8, n_tok), f32), V((n_b, 8, n_tok), f32),
                V((rows, n_tok), bf), V((rows, ds_), bf),
                V((n_z, 2, n_y, rv, tok), f32), V((n_z, 2, n_y, rv, tok), bf),
                V((n_z, 2, n_y, rv, tok), bf),
                V((n_z1, n_off, 2, rv, tok), bf), V((n_z1, n_off, 2, rv, tok), bf),
                V((n_z1, rv, tok), bf), V((n_z1, rv, tok), bf),
                V((n_z2, n_y, rv, tok), bf), V((n_z2, n_y, rv, tok), bf),
                V((n_z2, n_off, rv, tok), bf), V((n_z2, n_off, rv, tok), bf),
                V((n_z, rv, tok), bf), V((n_z, rv, tok), bf), V((n_z, rv, tok), f32),
                V((rows, -(-scales.shape[1] // 8) * 8), f32), V((8, tok), f32),
                D((n_ch + 2,)), D((ds_ // 512,)), D((2,)), D((2,)),
                D((10, n_off, n_ch)), D((10, n_off, n_ch)),
                D((n_dp - 1,)), D((n_dp - 1,)), D((n_a,)), D((n_a,)), D((n_b,)), D((n_b,)),
                D((n_z,)), D((n_z,)), *[D((n_z, n_off))] * 4, D((n_z,)), D((n_z,)),
            ],
            compiler_params=pltpu.CompilerParams(
                collective_id=0, has_side_effects=True, vmem_limit_bytes=60 * 1024 * 1024
            ),
            name="distill",
        )(th_own, sh_own, codes, scales.T, weight, loss_scale)
        kl, gh, gw = hand_over(kl, gh, gw)
        return kl.reshape(tok), gh.T, gw

    in_specs = (
        P("dp", None),
        P("dp", None),
        P(("vocab", "dp"), None),
        P(("vocab", "dp"), None),
        P(("vocab", "dp"), None),
        P("dp"),
    )
    out_specs = (P("dp"), P("dp", "vocab"), P(("vocab", "dp"), None))
    return jax.shard_map(local, mesh=mesh, in_specs=in_specs, out_specs=out_specs, check_vma=False)
```

```python
import functools

import jax
import jax.numpy as jnp
from jax import lax
from jax.experimental import pallas as pl
from jax.experimental.pallas import tpu as pltpu
from jax.sharding import PartitionSpec as P

GROUP = 128
LANE = 128
MESH = pl.DeviceIdType.MESH


def step_width(cols):
    units = cols // 256
    per = max(k for k in (1, 2, 3, 5, 7) if units % k == 0)
    return per * 256


def dot_t(left_rows, right_rows):
    return lax.dot_general(
        left_rows, right_rows, (((1,), (1,)), ((), ())), preferred_element_type=jnp.float32
    )


def kernel(
    n_vocab, n_dp,
    th_own, sh_own, codes, scales, weight, loss_in,
    kl_out, gh_out, gw_out,
    th, sh, table, wgt, wgt_t, tlog, slog, lsc, stat, stat_b, fin, in_a, in_b,
    grad, gw_buf, mine, theirs, core_in,
    y1s, y1r, x1s, x1r, x2s, x2r, y2s, y2r, zs, zr, zf,
    sc_rows, loss_row, ld_sem, gw_sem, pc_s, pc_r, hop_s, hop_r,
    ls_s, ls_r, a_s, a_r, b_s, b_r, cs, cr, r1s, r1r, r2s, r2r, z_ss, z_rs,
):
    v, d = lax.axis_index("vocab"), lax.axis_index("dp")
    c, y = lax.rem(d, 2), lax.div(d, 2)
    p, q = lax.rem(v, 2), lax.div(v, 2)
    n_y, n_z = n_dp // 2, n_vocab // 2
    n_off = n_y - 1
    mate = 2 * y + 1 - c
    v_pair = 2 * q + 1 - p
    r = lax.rem(q, 2)
    v_quad = 2 * (q + 1 - 2 * r) + p
    tok = th_own.shape[0]
    rv = zr.shape[1]
    n_z1 = n_z // 2

    def rcopy(src, dst, send, recv, dev):
        return pltpu.make_async_remote_copy(
            src_ref=src, dst_ref=dst, send_sem=send, recv_sem=recv,
            device_id=dev, device_id_type=MESH,
        )

    chunks = []
    for own, scr, tab, acc in ((th_own, th, table, tlog), (sh_own, sh, wgt, slog)):
        width = step_width(own.shape[1])
        for base in range(0, own.shape[1], width):
            chunks.append((own, scr, tab, acc, base, width))
    n_ch = len(chunks)

    loads = []
    for k, (own, scr, tab, acc, base, width) in enumerate(chunks):
        src = codes if tab is table else weight
        cp = pltpu.make_async_copy(
            src.at[:, pl.ds(base, width)], tab.at[:, pl.ds(base, width)], ld_sem.at[k]
        )
        cp.start()
        loads.append(cp)
    own_rows = pl.ds(pl.multiple_of(d * tok, tok), tok)
    own_loads = [
        pltpu.make_async_copy(th_own, th.at[own_rows], ld_sem.at[n_ch]),
        pltpu.make_async_copy(sh_own, sh.at[own_rows], ld_sem.at[n_ch + 1]),
    ]
    for cp in own_loads:
        cp.start()

    peers_a = []
    for dv in range(2):
        for dd in range(n_dp):
            if dv or dd:
                peers_a.append((v if dv == 0 else v_pair, lax.rem(d + dd, n_dp)))
    from_a = []
    peers_b = [(2 * lax.rem(q + o, n_z) + p, d) for o in range(1, n_z)]
    barrier = pltpu.get_barrier_semaphore()
    for peer in peers_a + peers_b:
        pl.semaphore_signal(barrier, inc=1, device_id=peer, device_id_type=MESH)
    pl.semaphore_wait(barrier, len(peers_a) + len(peers_b))

    quarter = tok // 4

    def rows(block):
        return pl.ds(pl.multiple_of(block * tok, tok), tok)

    def region(k, block, piece, half=None):
        scr, base, width = chunks[k][1], chunks[k][4], chunks[k][5]
        first, size = block * tok + piece * quarter, quarter
        if half is not None:
            size = quarter // 2
            first += half * size
        return scr.at[pl.ds(pl.multiple_of(first, size), size), pl.ds(base, width)]

    A, B, C, E = 2 * r + p, 2 * r + 1 - p, 2 * (1 - r) + p, 2 * (1 - r) + 1 - p
    X, Z = (v_pair, d), (v_quad, d)
    Y_A, Y_E, X_A, Z_A, X_C, Z_B, D_A, D_B, D_C, D_E = range(10)

    def far_by_y(k):
        return k > 0 and k % 2 == 0

    def came(o):
        return lax.rem(y + n_y - o, n_y)

    def y_send(k, o, kind):
        own, base, width = chunks[k][0], chunks[k][4], chunks[k][5]
        piece = A if kind == Y_A else E
        src = own.at[pl.ds(pl.multiple_of(piece * quarter, quarter), quarter), pl.ds(base, width)]
        to = 2 * lax.rem(y + o, n_y) + c
        return rcopy(
            src, region(k, d, piece), hop_s.at[kind, o - 1, k], hop_r.at[kind, o - 1, k], (v, to)
        )

    def hop(kind, k, o, side, piece, dev, half=None):
        ref = region(k, 2 * came(o) + side, piece, half)
        return rcopy(ref, ref, hop_s.at[kind, o - 1, k], hop_r.at[kind, o - 1, k], dev)

    def to_mate(kind, k, o, piece):
        launch(hop(kind, k, o, c, piece, (v, mate)))

    def launch(cp):
        cp.start()
        sends.append(cp)

    def stage_y(k):
        for o in range(1, n_y):
            hop(Y_A, k, o, c, A, X).wait_recv()
            launch(hop(X_A, k, o, c, A, X))
            launch(hop(Z_A, k, o, c, A, Z))
            to_mate(D_A, k, o, A)

    def stage_xz(k):
        for o in range(1, n_y):
            hop(X_A, k, o, c, B, X).wait_recv()
            if not far_by_y(k):
                launch(hop(Z_B, k, o, c, B, Z, 1))
            to_mate(D_B, k, o, B)
            hop(Z_A, k, o, c, C, Z).wait_recv()
            if not far_by_y(k):
                launch(hop(X_C, k, o, c, C, X, 0))
            to_mate(D_C, k, o, C)

    def stage_far(k):
        for o in range(1, n_y):
            if far_by_y(k):
                hop(Y_E, k, o, c, E, X).wait_recv()
            else:
                hop(X_C, k, o, c, E, X, 0).wait_recv()
                hop(Z_B, k, o, c, E, Z, 1).wait_recv()
            to_mate(D_E, k, o, E)

    def stage_mate(k):
        for o in range(1, n_y):
            for kind, piece in ((D_A, A), (D_B, B), (D_C, C), (D_E, E)):
                hop(kind, k, o, 1 - c, piece, X).wait_recv()

    sends = []
    mate_copies = [
        rcopy(th_own, th.at[own_rows], pc_s.at[0], pc_r.at[0], (v, mate)),
        rcopy(sh_own, sh.at[own_rows], pc_s.at[1], pc_r.at[1], (v, mate)),
    ]
    for k in range(n_ch):
        for o in range(1, n_y):
            launch(y_send(k, o, Y_A))
            if far_by_y(k):
                launch(y_send(k, o, Y_E))
        if k == 0:
            for cp in mate_copies:
                cp.start()
    loss_copies = []
    loss_row[...] = jnp.broadcast_to(
        loss_in[...].astype(jnp.float32).reshape(1, tok), loss_row.shape
    )
    lsc[d] = loss_row[...]
    groups = scales.shape[0]
    pad = jnp.zeros((sc_rows.shape[1] - groups, LANE), jnp.float32)
    for b in range(0, scales.shape[1], LANE):
        sc_rows[pl.ds(b, LANE), :] = jnp.concatenate(
            [scales[:, pl.ds(b, LANE)], pad], axis=0
        ).T

    def product(k, chip, first):
        own, scr, tab, acc, base, width = chunks[k]
        two = pl.ds(pl.multiple_of(chip * 2 * tok, 2 * tok), 2 * tok)
        part = dot_t(tab[:, pl.ds(base, width)], scr[two, pl.ds(base, width)])
        if first:
            acc[:, two] = part
        else:
            acc[:, two] += part

    def prepare(k):
        own, scr, tab, acc, base, width = chunks[k]
        loads[k].wait()
        if tab is table:
            @pl.loop(0, table.shape[0] // 64)
            def _(i):
                rsl = pl.ds(pl.multiple_of(i * 64, 64), 64)
                sc = sc_rows[rsl, :]
                for g in range(width // GROUP):
                    lane = pl.ds(base + g * GROUP, GROUP)
                    col = (base + g * GROUP) // GROUP
                    wide = table[rsl, lane].astype(jnp.float32) * sc[:, col : col + 1]
                    table[rsl, lane] = wide.astype(jnp.bfloat16)

    for cp in own_loads:
        cp.wait()
    firsts = [k == 0 or chunks[k][3] is not chunks[k - 1][3] for k in range(n_ch)]
    lag = 3
    for k in range(n_ch + lag):
        if k < n_ch:
            prepare(k)
            stage_y(k)
        if 1 <= k <= n_ch:
            stage_xz(k - 1)
        if 2 <= k <= n_ch + 1:
            stage_far(k - 2)
        if k < n_ch:
            if k == 0:
                for which, (own, scr) in enumerate(((th_own, th), (sh_own, sh))):
                    land = scr.at[rows(mate)]
                    rcopy(own, land, pc_s.at[which], pc_r.at[which], (v, mate)).wait_recv()
            product(k, y, firsts[k])
        if k >= lag:
            stage_mate(k - lag)
            if n_y > 1:
                @pl.loop(1, n_y)
                def _(o):
                    product(k - lag, lax.rem(y + n_y - o, n_y), firsts[k - lag])
        if k == n_ch - 1:
            for dd in range(1, n_dp):
                cp = rcopy(
                    loss_row, lsc.at[d], ls_s.at[dd - 1], ls_r.at[dd - 1],
                    (v, lax.rem(d + dd, n_dp)),
                )
                cp.start()
                loss_copies.append(cp)

    n_tok = n_dp * tok

    @pl.loop(0, n_dp)
    def _(j):
        sl = pl.ds(pl.multiple_of(j * tok, tok), tok)
        t_max = jnp.max(tlog[:, sl], axis=0, keepdims=True)
        s_max = jnp.max(slog[:, sl], axis=0, keepdims=True)
        te = jnp.exp(tlog[:, sl] - t_max)
        t_sum = jnp.sum(te, axis=0, keepdims=True)
        x_sum = jnp.sum(te * (tlog[:, sl] - slog[:, sl]), axis=0, keepdims=True)
        tlog[:, sl] = te
        se = jnp.exp(slog[:, sl] - s_max)
        s_sum = jnp.sum(se, axis=0, keepdims=True)
        slog[:, sl] = se
        stat[:, sl] = jnp.concatenate(
            [t_max, t_sum, x_sum, s_max, s_sum, jnp.zeros((3, tok), jnp.float32)], axis=0
        )

    def merge(parts):
        t_top = functools.reduce(jnp.maximum, [x[0:1] for x in parts])
        s_top = functools.reduce(jnp.maximum, [x[3:4] for x in parts])
        t_sum = x_sum = s_sum = 0.0
        for x in parts:
            t_w = jnp.exp(x[0:1] - t_top)
            t_sum += x[1:2] * t_w
            x_sum += x[2:3] * t_w
            s_sum += x[4:5] * jnp.exp(x[3:4] - s_top)
        return t_top, t_sum, x_sum, s_top, s_sum

    for i, peer in enumerate(peers_a):
        cp = rcopy(stat, in_a.at[i], a_s.at[i], a_r.at[i], peer)
        cp.start()
        sends.append(cp)
    for b in range(0, wgt.shape[1], 256):
        wgt_t[pl.ds(b, 256), :] = wgt[:, pl.ds(b, 256)].T
    for i, peer in enumerate(peers_a):
        rcopy(stat, in_a.at[i], a_s.at[i], a_r.at[i], peer).wait_recv()
    stat_b[...] = jnp.concatenate(
        list(merge([stat[...]] + [in_a[i] for i in range(len(peers_a))]))
        + [jnp.zeros((3, n_tok), jnp.float32)], axis=0
    )
    for i, peer in enumerate(peers_b):
        cp = rcopy(stat_b, in_b.at[i], b_s.at[i], b_r.at[i], peer)
        cp.start()
        sends.append(cp)
    for dd in range(1, n_dp):
        other = lax.rem(d + n_dp - dd, n_dp)
        rcopy(loss_row, lsc.at[other], ls_s.at[dd - 1], ls_r.at[dd - 1], (v, mate)).wait_recv()
    for i, peer in enumerate(peers_b):
        rcopy(stat_b, in_b.at[i], b_s.at[i], b_r.at[i], peer).wait_recv()
    t_top, t_sum, x_sum, s_top, s_sum = merge(
        [stat_b[...]] + [in_b[i] for i in range(len(peers_b))]
    )
    t_lse = t_top + jnp.log(t_sum)
    s_lse = s_top + jnp.log(s_sum)
    fin[...] = jnp.concatenate(
        [
            x_sum / t_sum - t_lse + s_lse,
            jnp.exp(stat[0:1] - t_lse),
            jnp.exp(stat[3:4] - s_lse),
            jnp.zeros((5, n_tok), jnp.float32),
        ],
        axis=0,
    )
    kl_out[...] = fin[0:1, own_rows]

    @pl.loop(0, n_dp)
    def _(j):
        sl = pl.ds(pl.multiple_of(j * tok, tok), tok)
        f = fin[:, sl]
        grad[:, sl] = (
            lsc[j][0:1] * (slog[:, sl] * f[2:3] - tlog[:, sl] * f[1:2])
        ).astype(jnp.bfloat16)

    order = []
    for i in range(n_z1):
        order += [i, n_z1 + i]
    order += [i for i in range(n_z) if i not in order]

    def hidden_part(z):
        for pp in range(2):
            feat = wgt_t[pl.ds((2 * z + pp) * rv, rv), :]
            for yy in range(n_y):
                part = jnp.dot(
                    feat, grad[:, pl.ds(yy * 2 * tok, 2 * tok)],
                    preferred_element_type=jnp.float32,
                )
                left, right = part[:, :tok], part[:, tok:]
                mine[z, pp, yy] = jnp.where(c == 0, left, right)
                theirs[z, pp, yy] = jnp.where(c == 0, right, left).astype(jnp.bfloat16)

    def core_copy(z):
        return rcopy(theirs.at[z], core_in.at[z], cs.at[z], cr.at[z], (v, mate))

    def y1_copy(z, o):
        to = 2 * lax.rem(y + o, n_y) + c
        return rcopy(
            y1s.at[z, o - 1], y1r.at[z, o - 1], r1s.at[z, o - 1], r1r.at[z, o - 1], (v, to)
        )

    def x1_copy(z):
        return rcopy(x1s.at[z], x1r.at[z], r2s.at[z, 0], r2r.at[z, 0], (v_pair, d))

    def x2_copy(z):
        return rcopy(
            x2s.at[z - n_z1], x2r.at[z - n_z1], r1s.at[z, 0], r1r.at[z, 0], (v_pair, d)
        )

    def y2_copy(z, o):
        to = 2 * lax.rem(y + o, n_y) + c
        return rcopy(
            y2s.at[z - n_z1, o - 1], y2r.at[z - n_z1, o - 1],
            r2s.at[z, o - 1], r2r.at[z, o - 1], (v, to),
        )

    def after_core(z):
        core_copy(z).wait_recv()
        if z < n_z1:
            for o in range(1, n_y):
                to = lax.rem(y + o, n_y)
                for pp in range(2):
                    y1s[z, o - 1, pp] = (
                        mine[z, pp, to] + core_in[z, pp, to].astype(jnp.float32)
                    ).astype(jnp.bfloat16)
                launch(y1_copy(z, o))
        else:
            for yy in range(n_y):
                x2s[z - n_z1, yy] = (
                    mine[z, 1 - p, yy] + core_in[z, 1 - p, yy].astype(jnp.float32)
                ).astype(jnp.bfloat16)
            launch(x2_copy(z))

    def after_first(z):
        if z < n_z1:
            for o in range(1, n_y):
                y1_copy(z, o).wait_recv()

            def total(which):
                out = mine[z, which, y] + core_in[z, which, y].astype(jnp.float32)
                for o in range(1, n_y):
                    out += y1r[z, o - 1, which].astype(jnp.float32)
                return out

            x1s[z] = total(1 - p).astype(jnp.bfloat16)
            launch(x1_copy(z))
            zf[z] = total(p)
        else:
            x2_copy(z).wait_recv()

            def total(yy):
                return (
                    mine[z, p, yy] + core_in[z, p, yy].astype(jnp.float32)
                    + x2r[z - n_z1, yy].astype(jnp.float32)
                )

            for o in range(1, n_y):
                y2s[z - n_z1, o - 1] = total(lax.rem(y + o, n_y)).astype(jnp.bfloat16)
                launch(y2_copy(z, o))
            zf[z] = total(y)

    def z_copy(z):
        return rcopy(zs.at[z], zr.at[q], z_ss.at[z], z_rs.at[q], (2 * z + p, d))

    def after_second(z):
        if z < n_z1:
            x1_copy(z).wait_recv()
            full = zf[z] + x1r[z].astype(jnp.float32)
        else:
            full = zf[z]
            for o in range(1, n_y):
                y2_copy(z, o).wait_recv()
                full += y2r[z - n_z1, o - 1].astype(jnp.float32)
        zf[z] = full
        zs[z] = full.astype(jnp.bfloat16)

        @pl.when(q != z)
        def _():
            z_copy(z).start()

    n_gw = sh.shape[1] // 512
    gw_copies = []

    def weight_part(b):
        sl = pl.ds(b * 512, 512)
        gw_buf[:, sl] = jnp.dot(
            grad[...], sh[:, sl], preferred_element_type=jnp.float32
        ).astype(jnp.bfloat16)
        cp = pltpu.make_async_copy(gw_buf.at[:, sl], gw_out.at[:, sl], gw_sem.at[b])
        cp.start()
        gw_copies.append(cp)

    for z in order:
        hidden_part(z)
        launch(core_copy(z))
    for z in order:
        after_core(z)
    for b in range(n_gw):
        weight_part(b)
    for z in order:
        after_first(z)
    for z in order:
        after_second(z)
    zf_q = zf[q]
    mine_sum = [zf_q]
    total = zf_q
    for o in range(1, n_z):
        src = lax.rem(q + o, n_z)
        rcopy(zs.at[src], zr.at[src], z_ss.at[src], z_rs.at[src], (v_pair, d)).wait_recv()
        total += zr[src].astype(jnp.float32)
    gh_out[...] = total.astype(jnp.bfloat16)

    for cp in sends + loss_copies + mate_copies:
        cp.wait_send()
    for o in range(1, n_z):
        dst = lax.rem(q + o, n_z)
        rcopy(zs.at[dst], zr.at[q], z_ss.at[dst], z_rs.at[q], (2 * dst + p, d)).wait_send()
    for cp in gw_copies:
        cp.wait()


def hand_over(kl, gh, gw):
    parts = 4
    step = gw.shape[0] // parts

    def move(kl_in, gh_in, gw_in, kl_to, gh_to, gw_to, kl_v, gh_v, gw_v, sem_in, sem_out):
        plan = [(kl_in, kl_v, kl_to), (gh_in, gh_v, gh_to)]
        for i in range(parts):
            sl = pl.ds(i * step, step)
            plan.append((gw_in.at[sl], gw_v.at[sl], gw_to.at[sl]))
        reads = [pltpu.make_async_copy(a, b, sem_in.at[i]) for i, (a, b, _) in enumerate(plan)]
        writes = [pltpu.make_async_copy(b, e, sem_out.at[i]) for i, (_, b, e) in enumerate(plan)]
        for cp in reads:
            cp.start()
        for cp, out in zip(reads, writes):
            cp.wait()
            out.start()
        for out in writes:
            out.wait()

    spec = pl.BlockSpec(memory_space=pl.ANY)
    arrays = (kl, gh, gw)
    return pl.pallas_call(
        move,
        out_shape=tuple(jax.ShapeDtypeStruct(a.shape, a.dtype) for a in arrays),
        in_specs=[spec] * 3,
        out_specs=(spec,) * 3,
        scratch_shapes=[pltpu.VMEM(a.shape, a.dtype) for a in arrays]
        + [pltpu.SemaphoreType.DMA((parts + 2,))] * 2,
        name="hand_over",
    )(*arrays)


def solution(mesh):
    n_vocab, n_dp = mesh.shape["vocab"], mesh.shape["dp"]

    def local(th_own, sh_own, codes, scales, weight, loss_scale):
        tok, dt = th_own.shape
        ds_ = sh_own.shape[1]
        rows = codes.shape[0]
        n_tok = tok * n_dp
        n_y, n_z = n_dp // 2, n_vocab // 2
        n_off, n_z1 = n_y - 1, n_z // 2
        n_z2 = n_z - n_z1
        rv = ds_ // n_vocab
        n_ch = dt // step_width(dt) + ds_ // step_width(ds_)
        n_a, n_b = 2 * n_dp - 1, n_z - 1
        bf, f32 = jnp.bfloat16, jnp.float32
        V, D = pltpu.VMEM, pltpu.SemaphoreType.DMA
        any_spec = pl.BlockSpec(memory_space=pl.ANY)
        vm_spec = pl.BlockSpec(memory_space=pltpu.VMEM)
        kl, gh, gw = pl.pallas_call(
            functools.partial(kernel, n_vocab, n_dp),
            out_shape=(
                jax.ShapeDtypeStruct((1, tok), f32),
                jax.ShapeDtypeStruct((rv, tok), bf),
                jax.ShapeDtypeStruct((rows, ds_), bf),
            ),
            in_specs=[any_spec, any_spec, any_spec, vm_spec, any_spec, vm_spec],
            out_specs=(vm_spec, vm_spec, any_spec),
            scratch_shapes=[
                V((n_tok, dt), bf), V((n_tok, ds_), bf), V((rows, dt), bf), V((rows, ds_), bf),
                V((ds_, rows), bf), V((rows, n_tok), f32), V((rows, n_tok), f32),
                V((n_dp, 8, tok), f32), V((8, n_tok), f32), V((8, n_tok), f32),
                V((8, n_tok), f32), V((n_a, 8, n_tok), f32), V((n_b, 8, n_tok), f32),
                V((rows, n_tok), bf), V((rows, ds_), bf),
                V((n_z, 2, n_y, rv, tok), f32), V((n_z, 2, n_y, rv, tok), bf),
                V((n_z, 2, n_y, rv, tok), bf),
                V((n_z1, n_off, 2, rv, tok), bf), V((n_z1, n_off, 2, rv, tok), bf),
                V((n_z1, rv, tok), bf), V((n_z1, rv, tok), bf),
                V((n_z2, n_y, rv, tok), bf), V((n_z2, n_y, rv, tok), bf),
                V((n_z2, n_off, rv, tok), bf), V((n_z2, n_off, rv, tok), bf),
                V((n_z, rv, tok), bf), V((n_z, rv, tok), bf), V((n_z, rv, tok), f32),
                V((rows, -(-scales.shape[1] // 8) * 8), f32), V((8, tok), f32),
                D((n_ch + 2,)), D((ds_ // 512,)), D((2,)), D((2,)),
                D((10, n_off, n_ch)), D((10, n_off, n_ch)),
                D((n_dp - 1,)), D((n_dp - 1,)), D((n_a,)), D((n_a,)), D((n_b,)), D((n_b,)),
                D((n_z,)), D((n_z,)), *[D((n_z, n_off))] * 4, D((n_z,)), D((n_z,)),
            ],
            compiler_params=pltpu.CompilerParams(
                collective_id=0, has_side_effects=True, vmem_limit_bytes=60 * 1024 * 1024
            ),
            name="distill",
        )(th_own, sh_own, codes, scales.T, weight, loss_scale)
        kl, gh, gw = hand_over(kl, gh, gw)
        return kl.reshape(tok), gh.T, gw

    in_specs = (
        P("dp", None),
        P("dp", None),
        P(("vocab", "dp"), None),
        P(("vocab", "dp"), None),
        P(("vocab", "dp"), None),
        P("dp"),
    )
    out_specs = (P("dp"), P("dp", "vocab"), P(("vocab", "dp"), None))
    return jax.shard_map(local, mesh=mesh, in_specs=in_specs, out_specs=out_specs, check_vma=False)
```
